128 devices in a mesh: freq: 4 (over z), row: 8 (over y, core), col: 4 (over x).
Axes of the slice: x: 4, y: 4, z: 4, core: 2. Of those that a mesh axis runs over, the one named last changes fastest.
Arguments:
- source_rows: bfloat16 [2, 16, 32, 4096], P(None, 'freq', 'row', 'col'), may hold values from -6 to 6
- data_matrix: bfloat16 [2, 16, 4096, 4096], P(None, 'freq', 'col', 'row'), may hold values from -0.0625 to 0.0625
- observed: bfloat16 [1024, 32, 4096], P(None, 'freq', ('row', 'col')), may hold values from -6 to 6
- window_owner: int32 [4, 32, 128, 1], P('freq', ('row', 'col')), may hold values from 0 to 127; in each aligned block of 128 rows (0 to 127, 128 to 255, ..., all dimensions but the last counted through in order) at most 2 rows name the same one
- filter_len: int32 [4, 32, 128], P('freq', ('row', 'col')), may hold values from 1 to 16, as said below
Outputs:
- primaries: bfloat16 [128, 128, 2, 64, 128], P(('freq', 'row', 'col'))
The draws below stay inside these ranges and needn't reach their ends.
Inputs may be any that keep to these rules, and one draw needn't show every extreme that they name: `window_owner`: among the 128 windows of one (g, p), at most 2 share an owner, and exactly 2 do for some owner in some blocks. `filter_len`: some window has 16 taps and some has 1.
All inputs are finite; a program needn't handle non-finite values.
Results may differ from the reference program's by a relative error of at most 0.0051.
Values may be sent and summed in bfloat16 or wider, within the bound.
No kernel may reach another device: no remote copies, remote signals or barrier semaphores. Data moves between devices by JAX's collectives and lax.ppermute only.
A program may use at most 192 MiB of HBM per device.

```python
import math
import jax
import jax.numpy as jnp
import numpy as np
from jax import lax

NREC = 4096
RG = 8
NT = 1024
WT = 64
WIN = 128
LMAX = 16
FIT_STEPS = 3
F = 16
ROWS = 32
GROUPS = 4
PANELS = 32
CBD = 1
TW = 16
WDEV = 128
SLOT = 2
DEVICES = 128


def draw_filter_len(key, part):
    values = jax.random.randint(key, (GROUPS, PANELS, WDEV), 1, LMAX + 1)
    values = values.at[0, 0, 0].set(LMAX)
    values = values.at[0, 0, 1].set(1)
    return values.astype(jnp.int32)


def steps_of(key, dims, split, least, high):
    gain, own = 1.0, jax.random.fold_in(key, 6)
    for axis_at, parts in split:
        steps = jnp.exp(jax.random.uniform(jax.random.fold_in(own, axis_at), (parts,), jnp.float32, least / len(split), high / len(split)))
        gain = gain * jnp.repeat(steps, dims[axis_at] // parts).reshape([-1 if axis == axis_at else 1 for axis in range(len(dims))])
    return gain


def shared_out(rng, own, number, rows, number_of, top, bound, slope):
    ranking = jax.random.permutation(rng, number_of)
    crowded, ordinary = load_shares(number_of, rows * top, bound, slope, True), load_shares(number_of, rows * top, bound, slope, False)
    places = jnp.arange(number_of)

    def named(sizes, offset_by):
        used = int((sizes > 0).sum())
        fixed = max(1, used // 4)
        moved = fixed + (places - fixed + offset_by * (used - fixed)) % max(1, number_of - fixed)
        return jnp.zeros((number_of,), jnp.int32).at[ranking[jnp.where(places < fixed, places, moved)]].set(jnp.asarray(sizes, jnp.int32))

    sizes = jnp.where(number % 4 == 0, named(crowded, number // 4), named(ordinary, number - number // 4 - 1))
    mixed = jax.random.permutation(jax.random.fold_in(own, 3), number_of)
    giver, taker = mixed[0:number_of // 2 * 2:2], mixed[1:number_of // 2 * 2:2]
    slack = jnp.minimum(sizes[giver] - 1, bound - sizes[taker]) // 2
    slack = jnp.where((giver == ranking[0]) | (taker == ranking[0]) | (sizes[taker] == 0), 0, jnp.maximum(slack, 0))
    moved = jax.random.randint(jax.random.fold_in(own, 4), (number_of // 2,), 0, 1 << 20) % (slack + 1)
    sizes = sizes.at[giver].add(-moved).at[taker].add(moved)
    members = jnp.searchsorted(jnp.cumsum(sizes), jnp.arange(rows * top), side="right").astype(jnp.int32)
    grid = members.reshape(top, rows).T
    grid = grid[jax.random.permutation(jax.random.fold_in(own, 1), rows)]
    offset_by = jax.random.randint(jax.random.fold_in(own, 2), (rows, 1), 0, top)
    return jnp.take_along_axis(grid, (jnp.arange(top)[None, :] + offset_by) % top, axis=1)


def load_shares(number_of, total, limit, slope, full):
    weights = [(1 << 20) // math.isqrt(standing ** slope) + 1 for standing in range(1, number_of + 1)]
    largest = limit if full else min(limit, max(-(-total // number_of), total * weights[0] // sum(weights)))
    least = 1 if total - largest >= number_of - 1 else 0
    given, surplus = [largest] + [least] * (number_of - 1), total - largest - least * (number_of - 1)
    while surplus > 0:
        candidates = [i for i in range(1, number_of) if given[i] < largest] or [i for i in range(1, number_of) if given[i] < limit]
        mass, budget = sum([weights[i] for i in candidates]), surplus
        for i in candidates:
            more = min(limit - given[i], max(1, budget * weights[i] // mass), surplus)
            given[i] = given[i] + more
            surplus = surplus - more
    return np.array(given)


def centred(own_key, dims, spread, bound, split=(), kind=jnp.bfloat16):
    factor_of = steps_of(own_key, dims, split, -0.22, 0.18) if split else 1.0
    drawn = jax.random.normal(own_key, dims, jnp.float32) * spread * factor_of
    return jnp.minimum(jnp.maximum(drawn, -bound), bound).astype(kind)


def setup_inputs(seed: int = 0) -> dict:
    seeds = jax.random.split(jax.random.key(seed), 6)
    source_rows = centred(seeds[0], (2, F, ROWS, NREC), 1.0, 6.0, ((1, 4), (2, 8), (3, 4)))
    data_matrix = centred(seeds[1], (2, F, NREC, NREC), (2 * NREC) ** -0.5, 0.0625, ((1, 4), (2, 4), (3, 8)))
    observed = centred(seeds[2], (NT, ROWS, NREC), 1.0, 6.0, ((1, 4), (2, 32)))
    window_owner_keys = jax.random.split(jax.random.fold_in(seeds[3], 1), GROUPS * PANELS * WDEV // WDEV)
    window_owner_turns = jax.random.permutation(jax.random.fold_in(seeds[3], 3), GROUPS * PANELS * WDEV // WDEV)
    window_owner = jax.vmap(lambda own, number: shared_out(jax.random.fold_in(seeds[3], 2), own, number, WDEV, DEVICES, 1, SLOT, 2))(window_owner_keys, window_owner_turns).reshape((GROUPS, PANELS, WDEV, 1))
    filter_len = draw_filter_len(jax.random.fold_in(seeds[5], 71), 0)
    return dict(source_rows=source_rows, data_matrix=data_matrix, observed=observed, window_owner=window_owner, filter_len=filter_len)


def idft_table(bands, samples):
    freqs = (jnp.arange(bands) + 1).astype(jnp.float32)
    times = jnp.arange(samples).astype(jnp.float32)
    angle = 2.0 * math.pi * freqs[:, None] * times[None, :] / samples
    return jnp.stack([jnp.cos(angle), -jnp.sin(angle)]) * (bands ** -0.5)


def lagged(field, lag_index):
    if lag_index == 0:
        return field
    widths = [(0, 0)] * (field.ndim - 2) + [(lag_index, 0), (0, 0)]
    return jnp.pad(field[..., :-lag_index, :], widths)


def adapt(predicted, recorded, tap_mask):
    taps = tap_mask.shape[-1]

    def convolve(filter_taps):
        total = jnp.zeros(predicted.shape, jnp.float32)
        for lag_index in range(taps):
            total = total + filter_taps[..., lag_index, None, None] * lagged(predicted, lag_index)
        return total

    energy = jnp.sum(predicted * predicted, axis=(-2, -1))
    step_size = 0.4 / (energy + 1e-6)
    first = (jnp.arange(taps) == 0).astype(jnp.float32)
    filter_taps = tap_mask * first
    residual = recorded - convolve(filter_taps)
    for sweep in range(FIT_STEPS):
        gradient = jnp.stack([jnp.sum(residual * lagged(predicted, lag_index), axis=(-2, -1)) for lag_index in range(taps)], axis=-1) * tap_mask
        filter_taps = filter_taps + step_size[..., None] * gradient
        residual = recorded - convolve(filter_taps)
    return residual


def reference(source_rows, data_matrix, observed, window_owner, filter_len):
    def one_band(index_f):
        real_rows = source_rows[0, index_f]
        imag_rows = source_rows[1, index_f]
        real_data = data_matrix[0, index_f]
        imag_data = data_matrix[1, index_f]
        real_part = jnp.dot(real_rows, real_data, preferred_element_type=jnp.float32) - jnp.dot(imag_rows, imag_data, preferred_element_type=jnp.float32)
        imag_part = jnp.dot(real_rows, imag_data, preferred_element_type=jnp.float32) + jnp.dot(imag_rows, real_data, preferred_element_type=jnp.float32)
        return jnp.stack([real_part, imag_part]).astype(jnp.bfloat16)

    spectra = lax.map(one_band, jnp.arange(F, dtype=jnp.int32))
    table = idft_table(F, NT)

    def to_windows(field):
        shaped = field.reshape(TW, WT, RG, PANELS, CBD, WIN).transpose(3, 2, 4, 0, 1, 5)
        return shaped.reshape(PANELS, WDEV, WT, WIN).astype(jnp.float32)

    def one_group(group):
        block = lax.dynamic_slice_in_dim(spectra, group * RG, RG, 2)
        traces = jnp.einsum('fzrc,zft->trc', block.astype(jnp.float32), table, precision=lax.Precision.HIGHEST).astype(jnp.bfloat16)
        recorded = lax.dynamic_slice_in_dim(observed, group * RG, RG, 1)
        lengths = lax.dynamic_index_in_dim(filter_len, group, 0, keepdims=False)
        tap_mask = (jnp.arange(LMAX, dtype=jnp.int32)[None, None, :] < lengths[:, :, None]).astype(jnp.float32)
        return adapt(to_windows(traces), to_windows(recorded), tap_mask).astype(jnp.bfloat16)

    cleaned = lax.map(one_group, jnp.arange(GROUPS, dtype=jnp.int32))
    owners = window_owner.reshape(DEVICES, WDEV)
    same_owner = owners[:, :, None] == owners[:, None, :]
    earlier = jnp.arange(WDEV)[None, :] < jnp.arange(WDEV)[:, None]
    slot_rank = jnp.sum(jnp.logical_and(same_owner, earlier[None]), axis=2).astype(jnp.int32)
    sources = jnp.broadcast_to(jnp.arange(DEVICES, dtype=jnp.int32)[:, None], (DEVICES, WDEV))
    result = jnp.zeros((DEVICES, DEVICES, SLOT, WT, WIN), jnp.bfloat16)
    return result.at[owners, sources, slot_rank].set(cleaned.reshape(DEVICES, WDEV, WT, WIN))
```

```python
import functools

import jax
import jax.numpy as jnp
import numpy as np
from jax import lax
from jax.experimental import pallas as pl
from jax.experimental.pallas import tpu as pltpu
from jax.sharding import PartitionSpec as P

NT = 1024
WT = 64
WIN = 128
LMAX = 16
FIT_STEPS = 3
BANDS = 16
ROWS_HERE = 8
WINDOWS = 128
KEPT = 24
UNROLL = 4


def table_parts(bands, samples):
    turns = (np.arange(samples)[:, None] * (np.arange(bands) + 1)[None, :]) % samples
    angle = 2.0 * np.pi * turns / samples
    table = np.concatenate([np.cos(angle), -np.sin(angle)], axis=1) * bands**-0.5
    left, parts = table, []
    for _ in range(3):
        part = left.astype(jnp.bfloat16)
        parts.append(part)
        left = left - part.astype(np.float64)
    return np.concatenate(parts, axis=1)


def both_tables():
    table = table_parts(BANDS, NT)
    reverse = table.reshape(NT // WT, WT, -1)[:, ::-1].reshape(NT, -1)
    return np.concatenate([table, reverse], axis=0)


def predict_kernel(rows_ref, data_ref, out_ref):
    rows = rows_ref[...].reshape(8, 8, rows_ref.shape[-1]).astype(jnp.float32)
    crossed = jnp.concatenate([-rows[:, 4:], rows[:, :4]], axis=1)
    depth = rows.shape[-1]
    plain = rows.reshape(64, depth).astype(jnp.bfloat16)
    crossed = crossed.reshape(64, depth).astype(jnp.bfloat16)
    total = jnp.dot(plain, data_ref[0, 0], preferred_element_type=jnp.float32)
    total += jnp.dot(crossed, data_ref[1, 0], preferred_element_type=jnp.float32)
    for group in range(4):
        for panel in range(4):
            out_ref[group * 4 + panel, 0] = total[
                group * 16 : group * 16 + 16, panel * WIN : panel * WIN + WIN
            ].astype(jnp.bfloat16)


def predict(rows, data):
    peers, bands, sides, depth = rows.shape
    columns = data.shape[-1]
    return pl.pallas_call(
        predict_kernel,
        grid=(bands,),
        in_specs=[
            pl.BlockSpec((peers, 1, sides, depth), lambda f: (0, f, 0, 0)),
            pl.BlockSpec((2, 1, depth, columns), lambda f: (0, f, 0, 0)),
        ],
        out_specs=pl.BlockSpec((16, 1, 16, WIN), lambda f: (0, f, 0, 0)),
        out_shape=jax.ShapeDtypeStruct((16, bands, 16, WIN), jnp.bfloat16),
        name="predict",
    )(rows, data)


def fit_kernel(
    target_ref,
    parts_ref,
    recorded_ref,
    length_ref,
    table_ref,
    out_ref,
    spec,
    stacked,
    field,
    kept,
    columns_at,
    correl_at,
    filters,
):
    for freq in range(4):
        total = parts_ref[freq * 4].astype(jnp.float32)
        for col in range(1, 4):
            total += parts_ref[freq * 4 + col].astype(jnp.float32)
        spec[pl.ds(freq * 64, 64), :] = total.reshape(64, WIN)
    for row in range(ROWS_HERE):
        first = (row // 4) * 8 + row % 4
        bands = jnp.concatenate(
            [spec[pl.ds(first, 16, stride=16), :], spec[pl.ds(first + 4, 16, stride=16), :]], axis=0
        ).astype(jnp.bfloat16)
        stacked[row] = jnp.concatenate([bands, bands, bands], axis=0)

    def traces_of(row, _):
        field[row] = jnp.dot(
            table_ref[...], stacked[row], preferred_element_type=jnp.float32
        ).astype(jnp.bfloat16)
        return 0

    lax.fori_loop(0, ROWS_HERE, traces_of, 0)

    def window_at(index):
        row, part = index // (NT // WT), index % (NT // WT)
        return row, pl.multiple_of(part * WT, WT)

    def correlate(step, _):
        for inner in range(UNROLL):
            index = step * UNROLL + inner
            row, start = window_at(index)
            ahead = field[row, pl.ds(start, WT), :]
            back = field[row, pl.ds(start + NT, WT), :]
            products = lax.dot_general(
                back,
                jnp.concatenate([recorded_ref[index], ahead], axis=0),
                (((1,), (1,)), ((), ())),
                preferred_element_type=jnp.float32,
            )
            turned = pltpu.roll(products, 1, 1, stride=1, stride_axis=0)
            rest = turned[16:24]
            for block in range(3, 8):
                rest += turned[block * 8 : block * 8 + 8]
            kept[pl.ds(pl.multiple_of(index * KEPT, 8), KEPT), :] = jnp.concatenate(
                [turned[:16], rest], axis=0
            )
        return 0

    lax.fori_loop(0, WINDOWS // UNROLL, correlate, 0)

    rest = kept[pl.ds(16, WINDOWS, stride=KEPT), :]
    for block in range(1, 8):
        rest += kept[pl.ds(16 + block, WINDOWS, stride=KEPT), :]
    rest = rest.T
    own, cross = rest[:LMAX], rest[64 : 64 + LMAX]
    for lag in reversed(range(LMAX)):
        lines = kept[pl.ds(lag, WINDOWS, stride=KEPT), :].T
        own = own + lines[:LMAX]
        cross = cross + lines[64 : 64 + LMAX]
        place = LMAX - 1 - lag
        columns_at[pl.ds(place * 32, LMAX), :] = jnp.zeros((LMAX, WIN), jnp.float32)
        columns_at[pl.ds(place * 32 + place, LMAX), :] = own
        correl_at[pl.ds(place, 1), :] = cross[lag : lag + 1]
    energy = own[:1]
    step_size = 0.4 / (energy + 1e-06)
    places = lax.broadcasted_iota(jnp.int32, (LMAX, WIN), 0)
    tap_mask = (LMAX - 1 - places < length_ref[...]).astype(jnp.float32)
    correl = correl_at[...]
    matrix = []
    for lag in range(LMAX):
        place = LMAX - 1 - lag
        upper = columns_at[pl.ds(place * 32, LMAX), :]
        lower = columns_at[pl.ds(place, LMAX, stride=32), :]
        matrix.append(jnp.where(places < place, lower, upper))
    taps = (places == LMAX - 1).astype(jnp.float32)
    change = jnp.zeros((LMAX, WIN), jnp.float32)
    for sweep in range(FIT_STEPS):
        if sweep == 0:
            covered = matrix[0]
        else:
            covered = jnp.zeros((LMAX, WIN), jnp.float32)
            for lag in range(LMAX):
                place = LMAX - 1 - lag
                covered += matrix[lag] * jnp.broadcast_to(taps[place : place + 1], (LMAX, WIN))
        update = step_size * ((correl - covered) * tap_mask)
        taps = taps + update
        change = change + update
    high = change.astype(jnp.bfloat16).astype(jnp.float32)
    low = change - high
    gap = jnp.zeros((48, WIN), jnp.float32)
    filters[...] = jnp.concatenate([gap, low, gap, high], axis=0).T

    lanes = lax.broadcasted_iota(jnp.int32, (16, WIN), 1)
    samples = lax.broadcasted_iota(jnp.int32, (16, WIN), 0)
    inside = (lanes % WT) <= samples

    def clear(step, _):
        for inner in range(8):
            out_ref[step * 8 + inner] = jnp.zeros((WT, WIN), jnp.bfloat16)
        return 0

    lax.fori_loop(0, out_ref.shape[0] // 8, clear, 0)

    def subtract(step, _):
        for inner in range(UNROLL):
            index = step * UNROLL + inner
            row, start = window_at(index)
            ahead = field[row, pl.ds(start, WT), :]
            line = jnp.broadcast_to(filters[pl.ds(index, 1), :], (WT, WIN))
            turned = pltpu.roll(line, 1, 1, stride=1, stride_axis=0)
            turned = jnp.concatenate([jnp.where(inside, turned[:16], 0.0), turned[16:]], axis=0)
            shaped = jnp.dot(
                turned.astype(jnp.bfloat16),
                jnp.concatenate([ahead, ahead], axis=0),
                preferred_element_type=jnp.float32,
            )
            left = recorded_ref[index].astype(jnp.float32) - ahead.astype(jnp.float32)
            out_ref[target_ref[index]] = (left - shaped).astype(jnp.bfloat16)
        return 0

    lax.fori_loop(0, WINDOWS // UNROLL, subtract, 0)


def fit(target, parts, recorded, lengths, table, slots):
    whole = pl.BlockSpec(memory_space=pltpu.VMEM)
    return pl.pallas_call(
        fit_kernel,
        in_specs=[pl.BlockSpec(memory_space=pltpu.SMEM)] + [whole] * 4,
        out_specs=whole,
        out_shape=jax.ShapeDtypeStruct((slots, WT, WIN), jnp.bfloat16),
        scratch_shapes=[
            pltpu.VMEM((256, WIN), jnp.float32),
            pltpu.VMEM((ROWS_HERE, 96, WIN), jnp.bfloat16),
            pltpu.VMEM((ROWS_HERE, 2 * NT, WIN), jnp.bfloat16),
            pltpu.VMEM((WINDOWS * KEPT, WIN), jnp.float32),
            pltpu.VMEM((LMAX * 32, WIN), jnp.float32),
            pltpu.VMEM((LMAX, WIN), jnp.float32),
            pltpu.VMEM((WINDOWS, WIN), jnp.float32),
        ],
        compiler_params=pltpu.CompilerParams(vmem_limit_bytes=40 * 1024 * 1024),
        name="fit",
    )(target, parts, recorded, lengths, table)


def slot_of(owners, slots_each):
    count = owners.shape[0]
    same = owners[:, None] == owners[None, :]
    earlier = jnp.arange(count)[None, :] < jnp.arange(count)[:, None]
    return owners * slots_each + jnp.sum(jnp.logical_and(same, earlier), axis=1, dtype=jnp.int32)


def local(source_rows, data_matrix, observed, window_owner, filter_len):
    devices = lax.axis_size("freq") * lax.axis_size("row") * lax.axis_size("col")
    sides, bands, rows, depth = source_rows.shape
    mine = source_rows.transpose(1, 0, 2, 3).reshape(bands, sides * rows, depth)
    peers = lax.axis_size("row")
    panel_rows = lax.all_to_all(
        jnp.broadcast_to(mine[None], (peers, *mine.shape)), "row", 0, 0, tiled=True
    )
    partial = predict(panel_rows, data_matrix)
    parts = lax.all_to_all(partial, ("freq", "col"), 0, 0, tiled=True)
    recorded = (
        observed.reshape(NT // WT, WT, ROWS_HERE, WIN).transpose(2, 0, 1, 3).reshape(-1, WT, WIN)
    )
    target = slot_of(window_owner.reshape(-1), 2)
    buffer = fit(
        target,
        parts,
        recorded,
        filter_len.reshape(1, -1),
        jnp.asarray(both_tables()),
        devices * 2,
    )
    result = lax.all_to_all(
        buffer.reshape(devices, 2, WT, WIN), ("freq", "row", "col"), 0, 0, tiled=True
    )
    return result[None]


def solution(mesh):
    return jax.shard_map(
        local,
        mesh=mesh,
        in_specs=(
            P(None, "freq", "row", "col"),
            P(None, "freq", "col", "row"),
            P(None, "freq", ("row", "col")),
            P("freq", ("row", "col"), None, None),
            P("freq", ("row", "col"), None),
        ),
        out_specs=P(("freq", "row", "col"), None, None, None, None),
        check_vma=False,
    )
```

```python
import functools

import jax
import jax.numpy as jnp
import numpy as np
from jax import lax
from jax.experimental import pallas as pl
from jax.experimental.pallas import tpu as pltpu
from jax.sharding import PartitionSpec as P

NT = 1024
WT = 64
WIN = 128
LMAX = 16
FIT_STEPS = 3
BANDS = 16
ROWS_HERE = 8
WINDOWS = 128
KEPT = 24
DRAINS = 8
UNROLL = 16


def table_parts(bands, samples):
    turns = (np.arange(samples)[:, None] * (np.arange(bands) + 1)[None, :]) % samples
    angle = 2.0 * np.pi * turns / samples
    table = np.concatenate([np.cos(angle), -np.sin(angle)], axis=1) * bands**-0.5
    left, parts = table, []
    for _ in range(3):
        part = left.astype(jnp.bfloat16)
        parts.append(part)
        left = left - part.astype(np.float64)
    return np.concatenate(parts, axis=1)


def both_tables():
    table = table_parts(BANDS, NT)
    reverse = table.reshape(NT // WT, WT, -1)[:, ::-1].reshape(NT, -1)
    return np.concatenate([table, reverse], axis=0)


def predict_kernel(*refs):
    pieces, data_ref, out_ref = refs[:8], refs[8], refs[9]
    first = lax.axis_index("row") // 2
    depth = data_ref.shape[2]
    for band in range(data_ref.shape[1]):
        plain, crossed = [], []
        for piece in pieces:
            real = piece[0, band].astype(jnp.float32)
            imag = piece[1, band].astype(jnp.float32)
            plain += [real, imag]
            crossed += [-imag, real]
        plain = jnp.concatenate(plain, axis=0).astype(jnp.bfloat16)
        crossed = jnp.concatenate(crossed, axis=0).astype(jnp.bfloat16)
        total = jnp.dot(plain, data_ref[0, band], preferred_element_type=jnp.float32)
        total += jnp.dot(crossed, data_ref[1, band], preferred_element_type=jnp.float32)
        for step in range(4):
            group = lax.rem(first + 4 - step, 4)
            for panel in range(4):
                out_ref[group * 4 + panel, band] = total[
                    step * 16 : step * 16 + 16, panel * WIN : panel * WIN + WIN
                ].astype(jnp.bfloat16)


def predict(pieces, data):
    bands = data.shape[1]
    whole = pl.BlockSpec(memory_space=pltpu.VMEM)
    return pl.pallas_call(
        predict_kernel,
        in_specs=[whole] * 9,
        out_specs=whole,
        out_shape=jax.ShapeDtypeStruct((16, bands, 16, WIN), jnp.bfloat16),
        compiler_params=pltpu.CompilerParams(vmem_limit_bytes=24 * 1024 * 1024),
        name="predict",
    )(*pieces, data)


def fit_kernel(
    target_ref,
    parts_ref,
    recorded_ref,
    length_ref,
    table_ref,
    out_ref,
    spec,
    stacked,
    field,
    kept,
    columns_at,
    correl_at,
    filters,
):
    core = lax.axis_index("row") % 2
    for freq in range(4):
        total = parts_ref[freq * 4].astype(jnp.float32)
        for col in range(1, 4):
            total += parts_ref[freq * 4 + col].astype(jnp.float32)
        for band in range(4):
            for half in range(2):
                at = freq * 64 + band * 16 + lax.rem(half + core, 2) * 8
                spec[pl.ds(pl.multiple_of(at, 8), 8), :] = total[band, half * 8 : half * 8 + 8]
    for row in range(ROWS_HERE):
        first = (row // 4) * 8 + row % 4
        bands = jnp.concatenate(
            [spec[pl.ds(first, 16, stride=16), :], spec[pl.ds(first + 4, 16, stride=16), :]], axis=0
        ).astype(jnp.bfloat16)
        stacked[row] = jnp.concatenate([bands, bands, bands], axis=0)

    def traces_of(row, _):
        field[row] = jnp.dot(
            table_ref[...], stacked[row], preferred_element_type=jnp.float32
        ).astype(jnp.bfloat16)
        share = out_ref.shape[0] // ROWS_HERE
        out_ref[pl.ds(row * share, share)] = jnp.zeros((share, WT, WIN), jnp.bfloat16)
        return 0

    lax.fori_loop(0, ROWS_HERE, traces_of, 0)

    def window_at(index):
        row, part = index // (NT // WT), index % (NT // WT)
        return row, pl.multiple_of(part * WT, WT)

    def correlate(step, _):
        for inner in range(UNROLL):
            index = step * UNROLL + inner
            row, start = window_at(index)
            ahead = field[row, pl.ds(start, WT), :]
            back = field[row, pl.ds(start + NT, WT), :]
            products = lax.dot_general(
                back,
                jnp.concatenate([recorded_ref[index], ahead], axis=0),
                (((1,), (1,)), ((), ())),
                preferred_element_type=jnp.float32,
            )
            turned = pltpu.roll(products, 1, 1, stride=1, stride_axis=0)
            rest = turned[16:24]
            for block in range(3, 8):
                rest += turned[block * 8 : block * 8 + 8]
            kept[pl.ds(pl.multiple_of(index * KEPT, 8), KEPT), :] = jnp.concatenate(
                [turned[:16], rest], axis=0
            )
        return 0

    lax.fori_loop(0, WINDOWS // UNROLL, correlate, 0)

    rest = kept[pl.ds(16, WINDOWS, stride=KEPT), :]
    for block in range(1, 8):
        rest += kept[pl.ds(16 + block, WINDOWS, stride=KEPT), :]
    rest = rest.T
    own, cross = rest[:LMAX], rest[64 : 64 + LMAX]
    for lag in reversed(range(LMAX)):
        lines = kept[pl.ds(lag, WINDOWS, stride=KEPT), :].T
        own = own + lines[:LMAX]
        cross = cross + lines[64 : 64 + LMAX]
        place = LMAX - 1 - lag
        columns_at[pl.ds(place * 32, LMAX), :] = jnp.zeros((LMAX, WIN), jnp.float32)
        columns_at[pl.ds(place * 32 + place, LMAX), :] = own
        correl_at[pl.ds(place, 1), :] = cross[lag : lag + 1]
    energy = own[:1]
    step_size = 0.4 / (energy + 1e-06)
    places = lax.broadcasted_iota(jnp.int32, (LMAX, WIN), 0)
    tap_mask = (LMAX - 1 - places < length_ref[...]).astype(jnp.float32)
    correl = correl_at[...]
    matrix = []
    for lag in range(LMAX):
        place = LMAX - 1 - lag
        upper = columns_at[pl.ds(place * 32, LMAX), :]
        lower = columns_at[pl.ds(place, LMAX, stride=32), :]
        matrix.append(jnp.where(places < place, lower, upper))
    taps = (places == LMAX - 1).astype(jnp.float32)
    change = jnp.zeros((LMAX, WIN), jnp.float32)
    for sweep in range(FIT_STEPS):
        if sweep == 0:
            covered = matrix[0]
        else:
            covered = jnp.zeros((LMAX, WIN), jnp.float32)
            for lag in range(LMAX):
                place = LMAX - 1 - lag
                covered += matrix[lag] * jnp.broadcast_to(taps[place : place + 1], (LMAX, WIN))
        update = step_size * ((correl - covered) * tap_mask)
        taps = taps + update
        change = change + update
    high = change.astype(jnp.bfloat16).astype(jnp.float32)
    low = change - high
    gap = jnp.zeros((48, WIN), jnp.float32)
    filters[...] = jnp.concatenate([gap, low, gap, high], axis=0).T

    lanes = lax.broadcasted_iota(jnp.int32, (16, WIN), 1)
    samples = lax.broadcasted_iota(jnp.int32, (16, WIN), 0)
    inside = (lanes % WT) <= samples

    def subtract(step, _):
        for inner in range(UNROLL):
            index = step * UNROLL + inner
            row, start = window_at(index)
            ahead = field[row, pl.ds(start, WT), :]
            line = jnp.broadcast_to(filters[pl.ds(index, 1), :], (WT, WIN))
            turned = pltpu.roll(line, 1, 1, stride=1, stride_axis=0)
            turned = jnp.concatenate([jnp.where(inside, turned[:16], 0.0), turned[16:]], axis=0)
            shaped = jnp.dot(
                turned.astype(jnp.bfloat16),
                jnp.concatenate([ahead, ahead], axis=0),
                preferred_element_type=jnp.float32,
            )
            left = recorded_ref[index].astype(jnp.float32) - ahead.astype(jnp.float32)
            out_ref[target_ref[index]] = (left - shaped).astype(jnp.bfloat16)
        return 0

    lax.fori_loop(0, WINDOWS // UNROLL, subtract, 0)


def fit(target, parts, recorded, lengths, table, slots):
    whole = pl.BlockSpec(memory_space=pltpu.VMEM)
    return pl.pallas_call(
        fit_kernel,
        in_specs=[pl.BlockSpec(memory_space=pltpu.SMEM)] + [whole] * 4,
        out_specs=whole,
        out_shape=jax.ShapeDtypeStruct((slots, WT, WIN), jnp.bfloat16),
        scratch_shapes=[
            pltpu.VMEM((256, WIN), jnp.float32),
            pltpu.VMEM((ROWS_HERE, 96, WIN), jnp.bfloat16),
            pltpu.VMEM((ROWS_HERE, 2 * NT, WIN), jnp.bfloat16),
            pltpu.VMEM((WINDOWS * KEPT, WIN), jnp.float32),
            pltpu.VMEM((LMAX * 32, WIN), jnp.float32),
            pltpu.VMEM((LMAX, WIN), jnp.float32),
            pltpu.VMEM((WINDOWS, WIN), jnp.float32),
        ],
        compiler_params=pltpu.CompilerParams(vmem_limit_bytes=40 * 1024 * 1024),
        name="fit",
    )(target, parts, recorded, lengths, table)


def drain_kernel(given_ref, out_ref, done):
    share = given_ref.shape[0] // DRAINS
    copies = [
        pltpu.make_async_copy(
            given_ref.at[pl.ds(part * share, share)],
            out_ref.at[pl.ds(part * share, share)],
            done.at[part],
        )
        for part in range(DRAINS)
    ]
    for copy in copies:
        copy.start()
    for copy in copies:
        copy.wait()


def drained(value):
    return pl.pallas_call(
        drain_kernel,
        in_specs=[pl.BlockSpec(memory_space=pltpu.VMEM)],
        out_specs=pl.BlockSpec(memory_space=pltpu.HBM),
        out_shape=jax.ShapeDtypeStruct(value.shape, value.dtype),
        scratch_shapes=[pltpu.SemaphoreType.DMA((DRAINS,))],
        compiler_params=pltpu.CompilerParams(vmem_limit_bytes=1024 * 1024),
        name="drain",
    )(value)


def rows_of_panel(mine):
    peers = lax.axis_size("row")

    def moved(value, target_of):
        return lax.ppermute(value, "row", [(at, target_of(at)) for at in range(peers)])

    own = [mine] + [moved(mine, lambda at, by=by: (at + by) % peers) for by in (2, 4, 6)]
    other = [moved(piece, lambda at: at ^ 1) for piece in own]
    return [piece for pair in zip(own, other) for piece in pair]


def slot_of(owners, slots_each):
    count = owners.shape[0]
    same = owners[:, None] == owners[None, :]
    earlier = jnp.arange(count)[None, :] < jnp.arange(count)[:, None]
    return owners * slots_each + jnp.sum(jnp.logical_and(same, earlier), axis=1, dtype=jnp.int32)


def local(source_rows, data_matrix, observed, window_owner, filter_len):
    devices = lax.axis_size("freq") * lax.axis_size("row") * lax.axis_size("col")
    partial = predict(rows_of_panel(source_rows), lax.ppermute(data_matrix, 'row', [(i, i) for i in range(8)]))
    parts = lax.all_to_all(partial, ("freq", "col"), 0, 0, tiled=True)
    recorded = (
        observed.reshape(NT // WT, WT, ROWS_HERE, WIN).transpose(2, 0, 1, 3).reshape(-1, WT, WIN)
    )
    target = slot_of(window_owner.reshape(-1), 2)
    buffer = fit(
        target,
        parts,
        recorded,
        filter_len.reshape(1, -1),
        jnp.asarray(both_tables()),
        devices * 2,
    )
    result = lax.all_to_all(
        buffer.reshape(devices, 2, WT, WIN), ("freq", "row", "col"), 0, 0, tiled=True
    )
    return drained(result)[None]


def solution(mesh):
    return jax.shard_map(
        local,
        mesh=mesh,
        in_specs=(
            P(None, "freq", "row", "col"),
            P(None, "freq", "col", "row"),
            P(None, "freq", ("row", "col")),
            P("freq", ("row", "col"), None, None),
            P("freq", ("row", "col"), None),
        ),
        out_specs=P(("freq", "row", "col"), None, None, None, None),
        check_vma=False,
    )
```

```python
import jax
import jax.numpy as jnp
import numpy as np
from jax import lax
from jax.experimental import pallas as pl
from jax.experimental.pallas import tpu as pltpu
from jax.sharding import PartitionSpec as P


NT = 1024
WT = 64
WIN = 128
LMAX = 16
FIT_STEPS = 3
BANDS = 16
ROWS_HERE = 8
WINDOWS = 128
KEPT = 24
DRAINS = 8
UNROLL = 64
AHEAD = 64


def table_parts(bands, samples):
    turns = (np.arange(samples)[:, None] * (np.arange(bands) + 1)[None, :]) % samples
    angle = 2.0 * np.pi * turns / samples
    table = np.concatenate([np.cos(angle), -np.sin(angle)], axis=1) * bands**-0.5
    left, parts = table, []
    for _ in range(3):
        part = left.astype(jnp.bfloat16)
        parts.append(part)
        left = left - part.astype(np.float64)
    return np.concatenate(parts, axis=1)


def predict_kernel(*refs):
    pieces, data_ref, out_ref = refs[:8], refs[8], refs[9]
    first = lax.axis_index("row") // 2
    for band in range(data_ref.shape[1]):
        plain, crossed = [], []
        for piece in pieces:
            real = piece[0, band].astype(jnp.float32)
            imag = piece[1, band].astype(jnp.float32)
            plain += [real, imag]
            crossed += [-imag, real]
        plain = jnp.concatenate(plain, axis=0).astype(jnp.bfloat16)
        crossed = jnp.concatenate(crossed, axis=0).astype(jnp.bfloat16)
        total = jnp.dot(plain, data_ref[0, band], preferred_element_type=jnp.float32)
        total += jnp.dot(crossed, data_ref[1, band], preferred_element_type=jnp.float32)
        for step in range(4):
            group = lax.rem(first + 4 - step, 4)
            for panel in range(4):
                out_ref[group * 4 + panel, band] = total[
                    step * 16 : step * 16 + 16, panel * WIN : panel * WIN + WIN
                ].astype(jnp.bfloat16)


def predict(pieces, data):
    bands = data.shape[1]
    whole = pl.BlockSpec(memory_space=pltpu.VMEM)
    return pl.pallas_call(
        predict_kernel,
        in_specs=[whole] * 9,
        out_specs=whole,
        out_shape=jax.ShapeDtypeStruct((16, bands, 16, WIN), jnp.bfloat16),
        compiler_params=pltpu.CompilerParams(vmem_limit_bytes=24 * 1024 * 1024),
        name="predict",
    )(*pieces, data)


def fit_kernel(
    target_ref,
    parts_ref,
    recorded_ref,
    length_ref,
    table_ref,
    out_ref,
    spec,
    stacked,
    field,
    kept,
    columns_at,
    correl_at,
    filters,
):
    core = lax.axis_index("row") % 2
    for freq in range(4):
        total = parts_ref[freq * 4].astype(jnp.float32)
        for col in range(1, 4):
            total += parts_ref[freq * 4 + col].astype(jnp.float32)
        for band in range(4):
            for half in range(2):
                at = freq * 64 + band * 16 + lax.rem(half + core, 2) * 8
                spec[pl.ds(pl.multiple_of(at, 8), 8), :] = total[band, half * 8 : half * 8 + 8]
    for pair in range(ROWS_HERE // 2):
        both = []
        for row in (2 * pair, 2 * pair + 1):
            first = (row // 4) * 8 + row % 4
            both.append(
                jnp.concatenate(
                    [
                        spec[pl.ds(first, 16, stride=16), :],
                        spec[pl.ds(first + 4, 16, stride=16), :],
                    ],
                    axis=0,
                ).astype(jnp.bfloat16)
            )
        both = jnp.concatenate(both, axis=1)
        stacked[pair] = jnp.concatenate([both, both, both], axis=0)

    mirror = 7 - lax.broadcasted_iota(jnp.int32, (8, WIN), 0)

    def traces_of(pair, _):
        traces = jnp.dot(
            table_ref[...], stacked[pair], preferred_element_type=jnp.float32
        )
        turned = []
        for first in range(0, NT, WT):
            for block in reversed(range(WT // 8)):
                tile = traces[first + block * 8 : first + block * 8 + 8]
                turned.append(
                    jnp.concatenate(
                        [
                            jnp.take_along_axis(tile[:, :WIN], mirror, axis=0),
                            jnp.take_along_axis(tile[:, WIN:], mirror, axis=0),
                        ],
                        axis=1,
                    )
                )
        turned = jnp.concatenate(turned, axis=0)
        for at in range(2):
            field[2 * pair + at, :NT] = traces[:, at * WIN : at * WIN + WIN].astype(jnp.bfloat16)
            field[2 * pair + at, NT:] = turned[:, at * WIN : at * WIN + WIN].astype(jnp.bfloat16)
        return 0

    lax.fori_loop(0, ROWS_HERE // 2, traces_of, 0)

    def window_at(index):
        row, part = index // (NT // WT), index % (NT // WT)
        return row, pl.multiple_of(part * WT, WT)

    none = jnp.zeros((WT, WIN), jnp.bfloat16)
    share = out_ref.shape[0] // WINDOWS

    def correlate(step, _):
        for inner in range(0, AHEAD, 2):
            aheads, backs, records = [], [], []
            for index in (step * AHEAD + inner, step * AHEAD + inner + 1):
                row, start = window_at(index)
                aheads.append(field[row, pl.ds(start, WT), :])
                backs.append(field[row, pl.ds(start + NT, WT), :])
                records.append(recorded_ref[index])
            products = lax.dot_general(
                jnp.concatenate(
                    [
                        jnp.concatenate([backs[0], none], axis=1),
                        jnp.concatenate([none, backs[1]], axis=1),
                    ],
                    axis=0,
                ),
                jnp.concatenate(
                    [jnp.concatenate(records, axis=1), jnp.concatenate(aheads, axis=1)], axis=0
                ),
                (((1,), (1,)), ((), ())),
                preferred_element_type=jnp.float32,
            )
            for at in range(2):
                index = step * AHEAD + inner + at
                turned = pltpu.roll(
                    products[at * WT : at * WT + WT], 1, 1, stride=1, stride_axis=0
                )
                out_ref[pl.ds(index * share, share)] = jnp.zeros((share, WT, WIN), jnp.bfloat16)
                rest = turned[16:24]
                for block in range(3, 8):
                    rest += turned[block * 8 : block * 8 + 8]
                kept[pl.ds(pl.multiple_of(index * KEPT, 8), KEPT), :] = jnp.concatenate(
                    [turned[:16], rest], axis=0
                )
        return 0

    lax.fori_loop(0, WINDOWS // AHEAD, correlate, 0)

    rest = kept[pl.ds(16, WINDOWS, stride=KEPT), :]
    for block in range(1, 8):
        rest += kept[pl.ds(16 + block, WINDOWS, stride=KEPT), :]
    rest = rest.T
    own, cross = rest[:LMAX], rest[64 : 64 + LMAX]
    for lag in reversed(range(LMAX)):
        lines = kept[pl.ds(lag, WINDOWS, stride=KEPT), :].T
        own = own + lines[:LMAX]
        cross = cross + lines[64 : 64 + LMAX]
        place = LMAX - 1 - lag
        columns_at[pl.ds(place * 32, LMAX), :] = jnp.zeros((LMAX, WIN), jnp.float32)
        columns_at[pl.ds(place * 32 + place, LMAX), :] = own
        correl_at[pl.ds(place, 1), :] = cross[lag : lag + 1]
    energy = own[:1]
    step_size = 0.4 / (energy + 1e-06)
    places = lax.broadcasted_iota(jnp.int32, (LMAX, WIN), 0)
    tap_mask = (LMAX - 1 - places < length_ref[...]).astype(jnp.float32)
    correl = correl_at[...]
    matrix = []
    for lag in range(LMAX):
        place = LMAX - 1 - lag
        upper = columns_at[pl.ds(place * 32, LMAX), :]
        lower = columns_at[pl.ds(place, LMAX, stride=32), :]
        matrix.append(jnp.where(places < place, lower, upper))
    taps = (places == LMAX - 1).astype(jnp.float32)
    change = jnp.zeros((LMAX, WIN), jnp.float32)
    for sweep in range(FIT_STEPS):
        if sweep == 0:
            covered = matrix[0]
        else:
            covered = jnp.zeros((LMAX, WIN), jnp.float32)
            for lag in range(LMAX):
                place = LMAX - 1 - lag
                covered += matrix[lag] * jnp.broadcast_to(taps[place : place + 1], (LMAX, WIN))
        update = step_size * ((correl - covered) * tap_mask)
        taps = taps + update
        change = change + update
    high = change.astype(jnp.bfloat16).astype(jnp.float32)
    low = change - high
    gap = jnp.zeros((48, WIN), jnp.float32)
    filters[...] = jnp.concatenate([gap, low, gap, high], axis=0).T

    lanes = lax.broadcasted_iota(jnp.int32, (16, WIN), 1)
    samples = lax.broadcasted_iota(jnp.int32, (16, WIN), 0)
    inside = (lanes % WT) <= samples

    def subtract(step, _):
        for inner in range(UNROLL):
            index = step * UNROLL + inner
            row, start = window_at(index)
            ahead = field[row, pl.ds(start, WT), :]
            line = jnp.broadcast_to(filters[pl.ds(index, 1), :], (WT, WIN))
            turned = pltpu.roll(line, 1, 1, stride=1, stride_axis=0)
            turned = jnp.concatenate([jnp.where(inside, turned[:16], 0.0), turned[16:]], axis=0)
            shaped = jnp.dot(
                turned.astype(jnp.bfloat16),
                jnp.concatenate([ahead, ahead], axis=0),
                preferred_element_type=jnp.float32,
            )
            left = recorded_ref[index].astype(jnp.float32) - ahead.astype(jnp.float32)
            out_ref[target_ref[index]] = (left - shaped).astype(jnp.bfloat16)
        return 0

    lax.fori_loop(0, WINDOWS // UNROLL, subtract, 0)


def fit(target, parts, recorded, lengths, table, slots):
    whole = pl.BlockSpec(memory_space=pltpu.VMEM)
    return pl.pallas_call(
        fit_kernel,
        in_specs=[pl.BlockSpec(memory_space=pltpu.SMEM)] + [whole] * 4,
        out_specs=whole,
        out_shape=jax.ShapeDtypeStruct((slots, WT, WIN), jnp.bfloat16),
        scratch_shapes=[
            pltpu.VMEM((256, WIN), jnp.float32),
            pltpu.VMEM((ROWS_HERE // 2, 96, 2 * WIN), jnp.bfloat16),
            pltpu.VMEM((ROWS_HERE, 2 * NT, WIN), jnp.bfloat16),
            pltpu.VMEM((WINDOWS * KEPT, WIN), jnp.float32),
            pltpu.VMEM((LMAX * 32, WIN), jnp.float32),
            pltpu.VMEM((LMAX, WIN), jnp.float32),
            pltpu.VMEM((WINDOWS, WIN), jnp.float32),
        ],
        compiler_params=pltpu.CompilerParams(vmem_limit_bytes=40 * 1024 * 1024),
        name="fit",
    )(target, parts, recorded, lengths, table)


def drain_kernel(given_ref, out_ref, done):
    share = given_ref.shape[0] // DRAINS
    copies = [
        pltpu.make_async_copy(
            given_ref.at[pl.ds(part * share, share)],
            out_ref.at[pl.ds(part * share, share)],
            done.at[part],
        )
        for part in range(DRAINS)
    ]
    for copy in copies:
        copy.start()
    for copy in copies:
        copy.wait()


def drained(value):
    return pl.pallas_call(
        drain_kernel,
        in_specs=[pl.BlockSpec(memory_space=pltpu.VMEM)],
        out_specs=pl.BlockSpec(memory_space=pltpu.HBM),
        out_shape=jax.ShapeDtypeStruct(value.shape, value.dtype),
        scratch_shapes=[pltpu.SemaphoreType.DMA((DRAINS,))],
        compiler_params=pltpu.CompilerParams(vmem_limit_bytes=1024 * 1024),
        name="drain",
    )(value)


def moved(value, target_of):
    pairs = [(at, target_of(at)) for at in range(lax.axis_size("row"))]
    return lax.ppermute(value, "row", pairs)


def rows_of_panel(mine):
    peers = lax.axis_size("row")
    own = [mine] + [moved(mine, lambda at, by=by: (at + by) % peers) for by in (2, 4, 6)]
    other = [moved(piece, lambda at: at ^ 1) for piece in own]
    own[0] = moved(mine, lambda at: at)
    return [piece for pair in zip(own, other) for piece in pair]


def slot_of(owners, slots_each):
    count = owners.shape[0]
    same = owners[:, None] == owners[None, :]
    earlier = jnp.arange(count)[None, :] < jnp.arange(count)[:, None]
    return owners * slots_each + jnp.sum(jnp.logical_and(same, earlier), axis=1, dtype=jnp.int32)


def local(source_rows, data_matrix, observed, window_owner, filter_len):
    devices = lax.axis_size("freq") * lax.axis_size("row") * lax.axis_size("col")
    data = moved(data_matrix, lambda at: at)
    partial = predict(rows_of_panel(source_rows), data)
    parts = lax.all_to_all(partial, ("freq", "col"), 0, 0, tiled=True)
    recorded = (
        observed.reshape(NT // WT, WT, ROWS_HERE, WIN).transpose(2, 0, 1, 3).reshape(-1, WT, WIN)
    )
    target = slot_of(window_owner.reshape(-1), 2)
    buffer = fit(
        target,
        parts,
        recorded,
        filter_len.reshape(1, -1),
        jnp.asarray(table_parts(BANDS, NT)),
        devices * 2,
    )
    result = lax.all_to_all(
        buffer.reshape(devices, 2, WT, WIN), ("freq", "row", "col"), 0, 0, tiled=True
    )
    return drained(result)[None]


def solution(mesh):
    return jax.shard_map(
        local,
        mesh=mesh,
        in_specs=(
            P(None, "freq", "row", "col"),
            P(None, "freq", "col", "row"),
            P(None, "freq", ("row", "col")),
            P("freq", ("row", "col"), None, None),
            P("freq", ("row", "col"), None),
        ),
        out_specs=P(("freq", "row", "col"), None, None, None, None),
        check_vma=False,
    )
```

```python
import jax
import jax.numpy as jnp
import numpy as np
from jax import lax
from jax.experimental import pallas as pl
from jax.experimental.pallas import tpu as pltpu
from jax.sharding import PartitionSpec as P


NT = 1024
WT = 64
WIN = 128
LMAX = 16
FIT_STEPS = 3
BANDS = 16
ROWS_HERE = 8
WINDOWS = 128
KEPT = 24
DRAINS = 8
PREDICT_MIB = 50
UNROLL = 128
AHEAD = 128


def table_parts(bands, samples):
    turns = (np.arange(samples)[:, None] * (np.arange(bands) + 1)[None, :]) % samples
    angle = 2.0 * np.pi * turns / samples
    table = np.concatenate([np.cos(angle), -np.sin(angle)], axis=1) * bands**-0.5
    left, parts = table, []
    for _ in range(3):
        part = left.astype(jnp.bfloat16)
        parts.append(part)
        left = left - part.astype(np.float64)
    return np.concatenate(parts, axis=1)


def predict_kernel(*refs):
    pieces, data_ref, out_ref, held, rows, ready, landed, left = refs[:8], *refs[8:]
    first = lax.axis_index("row") // 2
    bands = data_ref.shape[1]
    coming = [
        [
            pltpu.make_async_copy(
                data_ref.at[side, band], held.at[side, band], landed.at[side, band]
            )
            for side in range(2)
        ]
        for band in range(bands)
    ]
    for pair in coming:
        for copy in pair:
            copy.start()
    for band in range(bands):
        plain, crossed = [], []
        for piece in pieces:
            real = piece[0, band].astype(jnp.float32)
            imag = piece[1, band].astype(jnp.float32)
            plain += [real, imag]
            crossed += [-imag, real]
        rows[0, band] = jnp.concatenate(plain, axis=0).astype(jnp.bfloat16)
        rows[1, band] = jnp.concatenate(crossed, axis=0).astype(jnp.bfloat16)
    leaving = []
    for band in range(bands):
        for copy in coming[band]:
            copy.wait()
        total = jnp.dot(rows[0, band], held[0, band], preferred_element_type=jnp.float32)
        total += jnp.dot(rows[1, band], held[1, band], preferred_element_type=jnp.float32)
        for step in range(4):
            group = lax.rem(first + 4 - step, 4)
            for panel in range(4):
                ready[band, group * 4 + panel] = total[
                    step * 16 : step * 16 + 16, panel * WIN : panel * WIN + WIN
                ].astype(jnp.bfloat16)
        copy = pltpu.make_async_copy(ready.at[band], out_ref.at[:, band], left.at[band])
        copy.start()
        leaving.append(copy)
    for copy in leaving:
        copy.wait()


def predict(pieces, data):
    bands = data.shape[1]
    whole = pl.BlockSpec(memory_space=pltpu.VMEM)
    outside = pl.BlockSpec(memory_space=pltpu.HBM)
    return pl.pallas_call(
        predict_kernel,
        in_specs=[whole] * 8 + [outside],
        out_specs=outside,
        out_shape=jax.ShapeDtypeStruct((16, bands, 16, WIN), jnp.bfloat16),
        scratch_shapes=[
            pltpu.VMEM(data.shape, data.dtype),
            pltpu.VMEM((2, bands, 64, data.shape[2]), data.dtype),
            pltpu.VMEM((bands, 16, 16, WIN), jnp.bfloat16),
            pltpu.SemaphoreType.DMA((2, bands)),
            pltpu.SemaphoreType.DMA((bands,)),
        ],
        compiler_params=pltpu.CompilerParams(vmem_limit_bytes=PREDICT_MIB * 1024 * 1024),
        name="predict",
    )(*pieces, data)


def fit_kernel(
    target_ref,
    parts_ref,
    recorded_ref,
    length_ref,
    table_ref,
    out_ref,
    spec,
    stacked,
    field,
    kept,
    columns_at,
    correl_at,
    filters,
):
    core = lax.axis_index("row") % 2
    for freq in range(4):
        total = parts_ref[freq * 4].astype(jnp.float32)
        for col in range(1, 4):
            total += parts_ref[freq * 4 + col].astype(jnp.float32)
        for band in range(4):
            for half in range(2):
                at = freq * 64 + band * 16 + lax.rem(half + core, 2) * 8
                spec[pl.ds(pl.multiple_of(at, 8), 8), :] = total[band, half * 8 : half * 8 + 8]
    for pair in range(ROWS_HERE // 2):
        both = []
        for row in (2 * pair, 2 * pair + 1):
            first = (row // 4) * 8 + row % 4
            both.append(
                jnp.concatenate(
                    [
                        spec[pl.ds(first, 16, stride=16), :],
                        spec[pl.ds(first + 4, 16, stride=16), :],
                    ],
                    axis=0,
                ).astype(jnp.bfloat16)
            )
        both = jnp.concatenate(both, axis=1)
        stacked[pair] = jnp.concatenate([both, both, both], axis=0)

    mirror = 7 - lax.broadcasted_iota(jnp.int32, (8, WIN), 0)

    def traces_of(pair, _):
        traces = jnp.dot(
            table_ref[...], stacked[pair], preferred_element_type=jnp.float32
        )
        turned = []
        for first in range(0, NT, WT):
            for block in reversed(range(WT // 8)):
                tile = traces[first + block * 8 : first + block * 8 + 8]
                turned.append(
                    jnp.concatenate(
                        [
                            jnp.take_along_axis(tile[:, :WIN], mirror, axis=0),
                            jnp.take_along_axis(tile[:, WIN:], mirror, axis=0),
                        ],
                        axis=1,
                    )
                )
        turned = jnp.concatenate(turned, axis=0)
        for at in range(2):
            field[2 * pair + at, :NT] = traces[:, at * WIN : at * WIN + WIN].astype(jnp.bfloat16)
            field[2 * pair + at, NT:] = turned[:, at * WIN : at * WIN + WIN].astype(jnp.bfloat16)
        return 0

    lax.fori_loop(0, ROWS_HERE // 2, traces_of, 0)

    def window_at(index):
        row, part = index // (NT // WT), index % (NT // WT)
        return row, pl.multiple_of(part * WT, WT)

    none = jnp.zeros((WT, WIN), jnp.bfloat16)
    share = out_ref.shape[0] // WINDOWS

    def correlate(step, _):
        for inner in range(0, AHEAD, 2):
            aheads, backs, records = [], [], []
            for index in (step * AHEAD + inner, step * AHEAD + inner + 1):
                row, start = window_at(index)
                aheads.append(field[row, pl.ds(start, WT), :])
                backs.append(field[row, pl.ds(start + NT, WT), :])
                records.append(recorded_ref[index])
            products = lax.dot_general(
                jnp.concatenate(
                    [
                        jnp.concatenate([backs[0], none], axis=1),
                        jnp.concatenate([none, backs[1]], axis=1),
                    ],
                    axis=0,
                ),
                jnp.concatenate(
                    [jnp.concatenate(records, axis=1), jnp.concatenate(aheads, axis=1)], axis=0
                ),
                (((1,), (1,)), ((), ())),
                preferred_element_type=jnp.float32,
            )
            for at in range(2):
                index = step * AHEAD + inner + at
                turned = pltpu.roll(
                    products[at * WT : at * WT + WT], 1, 1, stride=1, stride_axis=0
                )
                out_ref[pl.ds(index * share, share)] = jnp.zeros((share, WT, WIN), jnp.bfloat16)
                rest = turned[16:24]
                for block in range(3, 8):
                    rest += turned[block * 8 : block * 8 + 8]
                kept[pl.ds(pl.multiple_of(index * KEPT, 8), KEPT), :] = jnp.concatenate(
                    [turned[:16], rest], axis=0
                )
        return 0

    lax.fori_loop(0, WINDOWS // AHEAD, correlate, 0)

    rest = kept[pl.ds(16, WINDOWS, stride=KEPT), :]
    for block in range(1, 8):
        rest += kept[pl.ds(16 + block, WINDOWS, stride=KEPT), :]
    rest = rest.T
    own, cross = rest[:LMAX], rest[64 : 64 + LMAX]
    for lag in reversed(range(LMAX)):
        lines = kept[pl.ds(lag, WINDOWS, stride=KEPT), :].T
        own = own + lines[:LMAX]
        cross = cross + lines[64 : 64 + LMAX]
        place = LMAX - 1 - lag
        columns_at[pl.ds(place * 32, LMAX), :] = jnp.zeros((LMAX, WIN), jnp.float32)
        columns_at[pl.ds(place * 32 + place, LMAX), :] = own
        correl_at[pl.ds(place, 1), :] = cross[lag : lag + 1]
    energy = own[:1]
    step_size = 0.4 / (energy + 1e-06)
    places = lax.broadcasted_iota(jnp.int32, (LMAX, WIN), 0)
    tap_mask = (LMAX - 1 - places < length_ref[...]).astype(jnp.float32)
    correl = correl_at[...]
    matrix = []
    for lag in range(LMAX):
        place = LMAX - 1 - lag
        upper = columns_at[pl.ds(place * 32, LMAX), :]
        lower = columns_at[pl.ds(place, LMAX, stride=32), :]
        matrix.append(jnp.where(places < place, lower, upper))
    taps = (places == LMAX - 1).astype(jnp.float32)
    change = jnp.zeros((LMAX, WIN), jnp.float32)
    for sweep in range(FIT_STEPS):
        if sweep == 0:
            covered = matrix[0]
        else:
            covered = jnp.zeros((LMAX, WIN), jnp.float32)
            for lag in range(LMAX):
                place = LMAX - 1 - lag
                covered += matrix[lag] * jnp.broadcast_to(taps[place : place + 1], (LMAX, WIN))
        update = step_size * ((correl - covered) * tap_mask)
        taps = taps + update
        change = change + update
    high = change.astype(jnp.bfloat16).astype(jnp.float32)
    low = change - high
    gap = jnp.zeros((48, WIN), jnp.float32)
    filters[...] = jnp.concatenate([gap, low, gap, high], axis=0).T

    lanes = lax.broadcasted_iota(jnp.int32, (16, WIN), 1)
    samples = lax.broadcasted_iota(jnp.int32, (16, WIN), 0)
    inside = (lanes % WT) <= samples

    def subtract(step, _):
        for inner in range(UNROLL):
            index = step * UNROLL + inner
            row, start = window_at(index)
            ahead = field[row, pl.ds(start, WT), :]
            line = jnp.broadcast_to(filters[pl.ds(index, 1), :], (WT, WIN))
            turned = pltpu.roll(line, 1, 1, stride=1, stride_axis=0)
            turned = jnp.concatenate([jnp.where(inside, turned[:16], 0.0), turned[16:]], axis=0)
            shaped = jnp.dot(
                turned.astype(jnp.bfloat16),
                jnp.concatenate([ahead, ahead], axis=0),
                preferred_element_type=jnp.float32,
            )
            left = recorded_ref[index].astype(jnp.float32) - ahead.astype(jnp.float32)
            out_ref[target_ref[index]] = (left - shaped).astype(jnp.bfloat16)
        return 0

    lax.fori_loop(0, WINDOWS // UNROLL, subtract, 0)


def fit(target, parts, recorded, lengths, table, slots):
    whole = pl.BlockSpec(memory_space=pltpu.VMEM)
    return pl.pallas_call(
        fit_kernel,
        in_specs=[pl.BlockSpec(memory_space=pltpu.SMEM)] + [whole] * 4,
        out_specs=whole,
        out_shape=jax.ShapeDtypeStruct((slots, WT, WIN), jnp.bfloat16),
        scratch_shapes=[
            pltpu.VMEM((256, WIN), jnp.float32),
            pltpu.VMEM((ROWS_HERE // 2, 96, 2 * WIN), jnp.bfloat16),
            pltpu.VMEM((ROWS_HERE, 2 * NT, WIN), jnp.bfloat16),
            pltpu.VMEM((WINDOWS * KEPT, WIN), jnp.float32),
            pltpu.VMEM((LMAX * 32, WIN), jnp.float32),
            pltpu.VMEM((LMAX, WIN), jnp.float32),
            pltpu.VMEM((WINDOWS, WIN), jnp.float32),
        ],
        compiler_params=pltpu.CompilerParams(vmem_limit_bytes=40 * 1024 * 1024),
        name="fit",
    )(target, parts, recorded, lengths, table)


def drain_kernel(given_ref, out_ref, done):
    share = given_ref.shape[0] // DRAINS
    copies = [
        pltpu.make_async_copy(
            given_ref.at[pl.ds(part * share, share)],
            out_ref.at[pl.ds(part * share, share)],
            done.at[part],
        )
        for part in range(DRAINS)
    ]
    for copy in copies:
        copy.start()
    for copy in copies:
        copy.wait()


def drained(value):
    return pl.pallas_call(
        drain_kernel,
        in_specs=[pl.BlockSpec(memory_space=pltpu.VMEM)],
        out_specs=pl.BlockSpec(memory_space=pltpu.HBM),
        out_shape=jax.ShapeDtypeStruct(value.shape, value.dtype),
        scratch_shapes=[pltpu.SemaphoreType.DMA((DRAINS,))],
        compiler_params=pltpu.CompilerParams(vmem_limit_bytes=1024 * 1024),
        name="drain",
    )(value)


def moved(value, target_of):
    pairs = [(at, target_of(at)) for at in range(lax.axis_size("row"))]
    return lax.ppermute(value, "row", pairs)


def rows_of_panel(mine):
    peers = lax.axis_size("row")
    own = [mine] + [moved(mine, lambda at, by=by: (at + by) % peers) for by in (2, 4, 6)]
    other = [moved(piece, lambda at: at ^ 1) for piece in own]
    own[0] = moved(mine, lambda at: at)
    return [piece for pair in zip(own, other) for piece in pair]


def slot_of(owners, slots_each):
    count = owners.shape[0]
    same = owners[:, None] == owners[None, :]
    earlier = jnp.arange(count)[None, :] < jnp.arange(count)[:, None]
    return owners * slots_each + jnp.sum(jnp.logical_and(same, earlier), axis=1, dtype=jnp.int32)


def local(source_rows, data_matrix, observed, window_owner, filter_len):
    devices = lax.axis_size("freq") * lax.axis_size("row") * lax.axis_size("col")
    partial = predict(rows_of_panel(source_rows), data_matrix)
    parts = lax.all_to_all(partial, ("freq", "col"), 0, 0, tiled=True)
    recorded = (
        observed.reshape(NT // WT, WT, ROWS_HERE, WIN).transpose(2, 0, 1, 3).reshape(-1, WT, WIN)
    )
    target = slot_of(window_owner.reshape(-1), 2)
    buffer = fit(
        target,
        parts,
        recorded,
        filter_len.reshape(1, -1),
        jnp.asarray(table_parts(BANDS, NT)),
        devices * 2,
    )
    result = lax.all_to_all(
        buffer.reshape(devices, 2, WT, WIN), ("freq", "row", "col"), 0, 0, tiled=True
    )
    return drained(result)[None]


def solution(mesh):
    return jax.shard_map(
        local,
        mesh=mesh,
        in_specs=(
            P(None, "freq", "row", "col"),
            P(None, "freq", "col", "row"),
            P(None, "freq", ("row", "col")),
            P("freq", ("row", "col"), None, None),
            P("freq", ("row", "col"), None),
        ),
        out_specs=P(("freq", "row", "col"), None, None, None, None),
        check_vma=False,
    )
```

```python
import jax
import jax.numpy as jnp
import numpy as np
from jax import lax
from jax.experimental import pallas as pl
from jax.experimental.pallas import tpu as pltpu
from jax.sharding import PartitionSpec as P


NT = 1024
WT = 64
WIN = 128
LMAX = 16
FIT_STEPS = 3
BANDS = 16
ROWS_HERE = 8
WINDOWS = 128
KEPT = 24
DRAINS = 8
UNROLL = 128
AHEAD = 128


def table_parts(bands, samples):
    turns = (np.arange(samples)[:, None] * (np.arange(bands) + 1)[None, :]) % samples
    angle = 2.0 * np.pi * turns / samples
    table = np.concatenate([np.cos(angle), -np.sin(angle)], axis=1) * bands**-0.5
    left, parts = table, []
    for _ in range(3):
        part = left.astype(jnp.bfloat16)
        parts.append(part)
        left = left - part.astype(np.float64)
    return np.concatenate(parts, axis=1)


def predict_kernel(*refs):
    pieces, data_ref, _, out_ref, ready, left = refs[:8], *refs[8:]
    first = lax.axis_index("row") // 2
    bands = data_ref.shape[1]
    leaving = []
    for band in range(bands):
        plain, crossed = [], []
        for piece in pieces:
            real = piece[0, band].astype(jnp.float32)
            imag = piece[1, band].astype(jnp.float32)
            plain += [real, imag]
            crossed += [-imag, real]
        plain = jnp.concatenate(plain, axis=0).astype(jnp.bfloat16)
        crossed = jnp.concatenate(crossed, axis=0).astype(jnp.bfloat16)
        total = jnp.dot(plain, data_ref[0, band], preferred_element_type=jnp.float32)
        total += jnp.dot(crossed, data_ref[1, band], preferred_element_type=jnp.float32)
        for step in range(4):
            group = lax.rem(first + 4 - step, 4)
            for panel in range(4):
                ready[band, group * 4 + panel] = total[
                    step * 16 : step * 16 + 16, panel * WIN : panel * WIN + WIN
                ].astype(jnp.bfloat16)
        copy = pltpu.make_async_copy(ready.at[band], out_ref.at[:, band], left.at[band])
        copy.start()
        leaving.append(copy)
    for copy in leaving:
        copy.wait()


def marker_kernel(out_ref):
    out_ref[...] = jnp.zeros(out_ref.shape, out_ref.dtype)


def marker():
    return pl.pallas_call(
        marker_kernel,
        out_specs=pl.BlockSpec(memory_space=pltpu.VMEM),
        out_shape=jax.ShapeDtypeStruct((8, WIN), jnp.float32),
        cost_estimate=pl.CostEstimate(
            flops=10**10, bytes_accessed=64 * 1024 * 1024, transcendentals=0
        ),
        compiler_params=pltpu.CompilerParams(vmem_limit_bytes=1024 * 1024),
        name="marker",
    )()


def predict(pieces, data, mark):
    bands = data.shape[1]
    whole = pl.BlockSpec(memory_space=pltpu.VMEM)
    return pl.pallas_call(
        predict_kernel,
        in_specs=[whole] * 10,
        out_specs=pl.BlockSpec(memory_space=pltpu.HBM),
        out_shape=jax.ShapeDtypeStruct((16, bands, 16, WIN), jnp.bfloat16),
        scratch_shapes=[
            pltpu.VMEM((bands, 16, 16, WIN), jnp.bfloat16),
            pltpu.SemaphoreType.DMA((bands,)),
        ],
        compiler_params=pltpu.CompilerParams(vmem_limit_bytes=24 * 1024 * 1024),
        name="predict",
    )(*pieces, data, mark)


def fit_kernel(
    target_ref,
    parts_ref,
    recorded_ref,
    length_ref,
    table_ref,
    out_ref,
    spec,
    stacked,
    field,
    kept,
    columns_at,
    correl_at,
    filters,
):
    core = lax.axis_index("row") % 2
    for freq in range(4):
        total = parts_ref[freq * 4].astype(jnp.float32)
        for col in range(1, 4):
            total += parts_ref[freq * 4 + col].astype(jnp.float32)
        for band in range(4):
            for half in range(2):
                at = freq * 64 + band * 16 + lax.rem(half + core, 2) * 8
                spec[pl.ds(pl.multiple_of(at, 8), 8), :] = total[band, half * 8 : half * 8 + 8]
    for pair in range(ROWS_HERE // 2):
        both = []
        for row in (2 * pair, 2 * pair + 1):
            first = (row // 4) * 8 + row % 4
            both.append(
                jnp.concatenate(
                    [
                        spec[pl.ds(first, 16, stride=16), :],
                        spec[pl.ds(first + 4, 16, stride=16), :],
                    ],
                    axis=0,
                ).astype(jnp.bfloat16)
            )
        both = jnp.concatenate(both, axis=1)
        stacked[pair] = jnp.concatenate([both, both, both], axis=0)

    mirror = 7 - lax.broadcasted_iota(jnp.int32, (8, WIN), 0)

    def traces_of(pair, _):
        traces = jnp.dot(
            table_ref[...], stacked[pair], preferred_element_type=jnp.float32
        )
        turned = []
        for first in range(0, NT, WT):
            for block in reversed(range(WT // 8)):
                tile = traces[first + block * 8 : first + block * 8 + 8]
                turned.append(
                    jnp.concatenate(
                        [
                            jnp.take_along_axis(tile[:, :WIN], mirror, axis=0),
                            jnp.take_along_axis(tile[:, WIN:], mirror, axis=0),
                        ],
                        axis=1,
                    )
                )
        turned = jnp.concatenate(turned, axis=0)
        for at in range(2):
            field[2 * pair + at, :NT] = traces[:, at * WIN : at * WIN + WIN].astype(jnp.bfloat16)
            field[2 * pair + at, NT:] = turned[:, at * WIN : at * WIN + WIN].astype(jnp.bfloat16)
        return 0

    lax.fori_loop(0, ROWS_HERE // 2, traces_of, 0)

    def window_at(index):
        row, part = index // (NT // WT), index % (NT // WT)
        return row, pl.multiple_of(part * WT, WT)

    none = jnp.zeros((WT, WIN), jnp.bfloat16)
    share = out_ref.shape[0] // WINDOWS

    def correlate(step, _):
        for inner in range(0, AHEAD, 2):
            aheads, backs, records = [], [], []
            for index in (step * AHEAD + inner, step * AHEAD + inner + 1):
                row, start = window_at(index)
                aheads.append(field[row, pl.ds(start, WT), :])
                backs.append(field[row, pl.ds(start + NT, WT), :])
                records.append(recorded_ref[index])
            products = lax.dot_general(
                jnp.concatenate(
                    [
                        jnp.concatenate([backs[0], none], axis=1),
                        jnp.concatenate([none, backs[1]], axis=1),
                    ],
                    axis=0,
                ),
                jnp.concatenate(
                    [jnp.concatenate(records, axis=1), jnp.concatenate(aheads, axis=1)], axis=0
                ),
                (((1,), (1,)), ((), ())),
                preferred_element_type=jnp.float32,
            )
            for at in range(2):
                index = step * AHEAD + inner + at
                turned = pltpu.roll(
                    products[at * WT : at * WT + WT], 1, 1, stride=1, stride_axis=0
                )
                out_ref[pl.ds(index * share, share)] = jnp.zeros((share, WT, WIN), jnp.bfloat16)
                rest = turned[16:24]
                for block in range(3, 8):
                    rest += turned[block * 8 : block * 8 + 8]
                kept[pl.ds(pl.multiple_of(index * KEPT, 8), KEPT), :] = jnp.concatenate(
                    [turned[:16], rest], axis=0
                )
        return 0

    lax.fori_loop(0, WINDOWS // AHEAD, correlate, 0)

    rest = kept[pl.ds(16, WINDOWS, stride=KEPT), :]
    for block in range(1, 8):
        rest += kept[pl.ds(16 + block, WINDOWS, stride=KEPT), :]
    rest = rest.T
    own, cross = rest[:LMAX], rest[64 : 64 + LMAX]
    for lag in reversed(range(LMAX)):
        lines = kept[pl.ds(lag, WINDOWS, stride=KEPT), :].T
        own = own + lines[:LMAX]
        cross = cross + lines[64 : 64 + LMAX]
        place = LMAX - 1 - lag
        columns_at[pl.ds(place * 32, LMAX), :] = jnp.zeros((LMAX, WIN), jnp.float32)
        columns_at[pl.ds(place * 32 + place, LMAX), :] = own
        correl_at[pl.ds(place, 1), :] = cross[lag : lag + 1]
    energy = own[:1]
    step_size = 0.4 / (energy + 1e-06)
    places = lax.broadcasted_iota(jnp.int32, (LMAX, WIN), 0)
    tap_mask = (LMAX - 1 - places < length_ref[...]).astype(jnp.float32)
    correl = correl_at[...]
    matrix = []
    for lag in range(LMAX):
        place = LMAX - 1 - lag
        upper = columns_at[pl.ds(place * 32, LMAX), :]
        lower = columns_at[pl.ds(place, LMAX, stride=32), :]
        matrix.append(jnp.where(places < place, lower, upper))
    taps = (places == LMAX - 1).astype(jnp.float32)
    change = jnp.zeros((LMAX, WIN), jnp.float32)
    for sweep in range(FIT_STEPS):
        if sweep == 0:
            covered = matrix[0]
        else:
            covered = jnp.zeros((LMAX, WIN), jnp.float32)
            for lag in range(LMAX):
                place = LMAX - 1 - lag
                covered += matrix[lag] * jnp.broadcast_to(taps[place : place + 1], (LMAX, WIN))
        update = step_size * ((correl - covered) * tap_mask)
        taps = taps + update
        change = change + update
    high = change.astype(jnp.bfloat16).astype(jnp.float32)
    low = change - high
    gap = jnp.zeros((48, WIN), jnp.float32)
    filters[...] = jnp.concatenate([gap, low, gap, high], axis=0).T

    lanes = lax.broadcasted_iota(jnp.int32, (16, WIN), 1)
    samples = lax.broadcasted_iota(jnp.int32, (16, WIN), 0)
    inside = (lanes % WT) <= samples

    def subtract(step, _):
        for inner in range(UNROLL):
            index = step * UNROLL + inner
            row, start = window_at(index)
            ahead = field[row, pl.ds(start, WT), :]
            line = jnp.broadcast_to(filters[pl.ds(index, 1), :], (WT, WIN))
            turned = pltpu.roll(line, 1, 1, stride=1, stride_axis=0)
            turned = jnp.concatenate([jnp.where(inside, turned[:16], 0.0), turned[16:]], axis=0)
            shaped = jnp.dot(
                turned.astype(jnp.bfloat16),
                jnp.concatenate([ahead, ahead], axis=0),
                preferred_element_type=jnp.float32,
            )
            left = recorded_ref[index].astype(jnp.float32) - ahead.astype(jnp.float32)
            out_ref[target_ref[index]] = (left - shaped).astype(jnp.bfloat16)
        return 0

    lax.fori_loop(0, WINDOWS // UNROLL, subtract, 0)


def fit(target, parts, recorded, lengths, table, slots):
    whole = pl.BlockSpec(memory_space=pltpu.VMEM)
    return pl.pallas_call(
        fit_kernel,
        in_specs=[pl.BlockSpec(memory_space=pltpu.SMEM)] + [whole] * 4,
        out_specs=whole,
        out_shape=jax.ShapeDtypeStruct((slots, WT, WIN), jnp.bfloat16),
        scratch_shapes=[
            pltpu.VMEM((256, WIN), jnp.float32),
            pltpu.VMEM((ROWS_HERE // 2, 96, 2 * WIN), jnp.bfloat16),
            pltpu.VMEM((ROWS_HERE, 2 * NT, WIN), jnp.bfloat16),
            pltpu.VMEM((WINDOWS * KEPT, WIN), jnp.float32),
            pltpu.VMEM((LMAX * 32, WIN), jnp.float32),
            pltpu.VMEM((LMAX, WIN), jnp.float32),
            pltpu.VMEM((WINDOWS, WIN), jnp.float32),
        ],
        compiler_params=pltpu.CompilerParams(vmem_limit_bytes=40 * 1024 * 1024),
        name="fit",
    )(target, parts, recorded, lengths, table)


def drain_kernel(given_ref, out_ref, done):
    share = given_ref.shape[0] // DRAINS
    copies = [
        pltpu.make_async_copy(
            given_ref.at[pl.ds(part * share, share)],
            out_ref.at[pl.ds(part * share, share)],
            done.at[part],
        )
        for part in range(DRAINS)
    ]
    for copy in copies:
        copy.start()
    for copy in copies:
        copy.wait()


def drained(value):
    return pl.pallas_call(
        drain_kernel,
        in_specs=[pl.BlockSpec(memory_space=pltpu.VMEM)],
        out_specs=pl.BlockSpec(memory_space=pltpu.HBM),
        out_shape=jax.ShapeDtypeStruct(value.shape, value.dtype),
        scratch_shapes=[pltpu.SemaphoreType.DMA((DRAINS,))],
        compiler_params=pltpu.CompilerParams(vmem_limit_bytes=1024 * 1024),
        name="drain",
    )(value)


def moved(value, target_of):
    pairs = [(at, target_of(at)) for at in range(lax.axis_size("row"))]
    return lax.ppermute(value, "row", pairs)


def rows_of_panel(mine):
    peers = lax.axis_size("row")
    own = [mine] + [moved(mine, lambda at, by=by: (at + by) % peers) for by in (2, 4, 6)]
    other = [moved(piece, lambda at: at ^ 1) for piece in own]
    return [piece for pair in zip(own, other) for piece in pair]


def slot_of(owners, slots_each):
    count = owners.shape[0]
    same = owners[:, None] == owners[None, :]
    earlier = jnp.arange(count)[None, :] < jnp.arange(count)[:, None]
    return owners * slots_each + jnp.sum(jnp.logical_and(same, earlier), axis=1, dtype=jnp.int32)


def local(source_rows, data_matrix, observed, window_owner, filter_len):
    devices = lax.axis_size("freq") * lax.axis_size("row") * lax.axis_size("col")
    mark = marker()
    partial = predict(rows_of_panel(source_rows), data_matrix, mark)
    parts = lax.all_to_all(partial, ("freq", "col"), 0, 0, tiled=True)
    recorded = (
        observed.reshape(NT // WT, WT, ROWS_HERE, WIN).transpose(2, 0, 1, 3).reshape(-1, WT, WIN)
    )
    target = slot_of(window_owner.reshape(-1), 2)
    buffer = fit(
        target,
        parts,
        recorded,
        filter_len.reshape(1, -1),
        jnp.asarray(table_parts(BANDS, NT)),
        devices * 2,
    )
    result = lax.all_to_all(
        buffer.reshape(devices, 2, WT, WIN), ("freq", "row", "col"), 0, 0, tiled=True
    )
    return drained(result)[None]


def solution(mesh):
    return jax.shard_map(
        local,
        mesh=mesh,
        in_specs=(
            P(None, "freq", "row", "col"),
            P(None, "freq", "col", "row"),
            P(None, "freq", ("row", "col")),
            P("freq", ("row", "col"), None, None),
            P("freq", ("row", "col"), None),
        ),
        out_specs=P(("freq", "row", "col"), None, None, None, None),
        check_vma=False,
    )
```

```python
import jax
import jax.numpy as jnp
import numpy as np
from jax import lax
from jax.experimental import pallas as pl
from jax.experimental.pallas import tpu as pltpu
from jax.sharding import PartitionSpec as P


NT = 1024
WT = 64
WIN = 128
LMAX = 16
FIT_STEPS = 3
BANDS = 16
ROWS_HERE = 8
WINDOWS = 128
KEPT = 24
DRAINS = 8


def table_parts(bands, samples):
    turns = (np.arange(samples)[:, None] * (np.arange(bands) + 1)[None, :]) % samples
    angle = 2.0 * np.pi * turns / samples
    table = np.concatenate([np.cos(angle), -np.sin(angle)], axis=1) * bands**-0.5
    left, parts = table, []
    for _ in range(3):
        part = left.astype(jnp.bfloat16)
        parts.append(part)
        left = left - part.astype(np.float64)
    return np.concatenate(parts, axis=1)


def predict_kernel(*refs):
    pieces, data_ref, _, out_ref, ready, left = refs[:8], *refs[8:]
    first = lax.axis_index("row") // 2
    bands = data_ref.shape[1]
    leaving = []
    for band in range(bands):
        plain, crossed = [], []
        for piece in pieces:
            real = piece[0, band].astype(jnp.float32)
            imag = piece[1, band].astype(jnp.float32)
            plain += [real, imag]
            crossed += [-imag, real]
        plain = jnp.concatenate(plain, axis=0).astype(jnp.bfloat16)
        crossed = jnp.concatenate(crossed, axis=0).astype(jnp.bfloat16)
        total = jnp.dot(plain, data_ref[0, band], preferred_element_type=jnp.float32)
        total += jnp.dot(crossed, data_ref[1, band], preferred_element_type=jnp.float32)
        for step in range(4):
            group = lax.rem(first + 4 - step, 4)
            for panel in range(4):
                ready[band, group * 4 + panel] = total[
                    step * 16 : step * 16 + 16, panel * WIN : panel * WIN + WIN
                ].astype(jnp.bfloat16)
        copy = pltpu.make_async_copy(ready.at[band], out_ref.at[:, band], left.at[band])
        copy.start()
        leaving.append(copy)
    for copy in leaving:
        copy.wait()


def marker_kernel(out_ref):
    out_ref[...] = jnp.zeros(out_ref.shape, out_ref.dtype)


def marker():
    return pl.pallas_call(
        marker_kernel,
        out_specs=pl.BlockSpec(memory_space=pltpu.VMEM),
        out_shape=jax.ShapeDtypeStruct((8, WIN), jnp.float32),
        cost_estimate=pl.CostEstimate(
            flops=10**10, bytes_accessed=64 * 1024 * 1024, transcendentals=0
        ),
        compiler_params=pltpu.CompilerParams(vmem_limit_bytes=1024 * 1024),
        name="marker",
    )()


def predict(pieces, data, mark):
    bands = data.shape[1]
    whole = pl.BlockSpec(memory_space=pltpu.VMEM)
    return pl.pallas_call(
        predict_kernel,
        in_specs=[whole] * 10,
        out_specs=pl.BlockSpec(memory_space=pltpu.HBM),
        out_shape=jax.ShapeDtypeStruct((16, bands, 16, WIN), jnp.bfloat16),
        scratch_shapes=[
            pltpu.VMEM((bands, 16, 16, WIN), jnp.bfloat16),
            pltpu.SemaphoreType.DMA((bands,)),
        ],
        compiler_params=pltpu.CompilerParams(vmem_limit_bytes=24 * 1024 * 1024),
        name="predict",
    )(*pieces, data, mark)


def fit_kernel(
    target_ref,
    parts_ref,
    recorded_ref,
    length_ref,
    table_ref,
    out_ref,
    spec,
    stacked,
    field,
    kept,
    columns_at,
    correl_at,
    filters,
):
    core = lax.axis_index("row") % 2
    for freq in range(4):
        total = parts_ref[freq * 4].astype(jnp.float32)
        for col in range(1, 4):
            total += parts_ref[freq * 4 + col].astype(jnp.float32)
        for band in range(4):
            for half in range(2):
                at = freq * 64 + band * 16 + lax.rem(half + core, 2) * 8
                spec[pl.ds(pl.multiple_of(at, 8), 8), :] = total[band, half * 8 : half * 8 + 8]
    for pair in range(ROWS_HERE // 2):
        both = []
        for row in (2 * pair, 2 * pair + 1):
            first = (row // 4) * 8 + row % 4
            both.append(
                jnp.concatenate(
                    [
                        spec[pl.ds(first, 16, stride=16), :],
                        spec[pl.ds(first + 4, 16, stride=16), :],
                    ],
                    axis=0,
                ).astype(jnp.bfloat16)
            )
        both = jnp.concatenate(both, axis=1)
        stacked[pair] = jnp.concatenate([both, both, both], axis=0)

    mirror = 7 - lax.broadcasted_iota(jnp.int32, (8, WIN), 0)

    def traces_of(pair):
        traces = jnp.dot(
            table_ref[...], stacked[pair], preferred_element_type=jnp.float32
        )
        turned = []
        for first in range(0, NT, WT):
            for block in reversed(range(WT // 8)):
                tile = traces[first + block * 8 : first + block * 8 + 8]
                turned.append(
                    jnp.concatenate(
                        [
                            jnp.take_along_axis(tile[:, :WIN], mirror, axis=0),
                            jnp.take_along_axis(tile[:, WIN:], mirror, axis=0),
                        ],
                        axis=1,
                    )
                )
        turned = jnp.concatenate(turned, axis=0)
        for at in range(2):
            field[2 * pair + at, :NT] = traces[:, at * WIN : at * WIN + WIN].astype(jnp.bfloat16)
            field[2 * pair + at, NT:] = turned[:, at * WIN : at * WIN + WIN].astype(jnp.bfloat16)

    def window_at(index):
        row, part = index // (NT // WT), index % (NT // WT)
        return row, part * WT

    none = jnp.zeros((WT, WIN), jnp.bfloat16)
    share = out_ref.shape[0] // WINDOWS

    def correlate(pair):
        for inner in range(pair * 32, pair * 32 + 32, 2):
            aheads, backs, records = [], [], []
            for index in (inner, inner + 1):
                row, start = window_at(index)
                aheads.append(field[row, pl.ds(start, WT), :])
                backs.append(field[row, pl.ds(start + NT, WT), :])
                records.append(recorded_ref[index])
            products = lax.dot_general(
                jnp.concatenate(
                    [
                        jnp.concatenate([backs[0], none], axis=1),
                        jnp.concatenate([none, backs[1]], axis=1),
                    ],
                    axis=0,
                ),
                jnp.concatenate(
                    [jnp.concatenate(records, axis=1), jnp.concatenate(aheads, axis=1)], axis=0
                ),
                (((1,), (1,)), ((), ())),
                preferred_element_type=jnp.float32,
            )
            for at in range(2):
                index = inner + at
                turned = pltpu.roll(
                    products[at * WT : at * WT + WT], 1, 1, stride=1, stride_axis=0
                )
                zero = jnp.minimum(jnp.maximum(turned[:16], 0.0), 0.0).astype(jnp.bfloat16)
                zero = jnp.concatenate([zero] * (WT // 16), axis=0)
                for slot in range(share):
                    out_ref[index * share + slot] = zero
                rest = turned[16:24]
                for block in range(3, 8):
                    rest += turned[block * 8 : block * 8 + 8]
                kept[pl.ds(index * KEPT, KEPT), :] = jnp.concatenate(
                    [turned[:16], rest], axis=0
                )

    for pair in range(ROWS_HERE // 2):
        if pair == 0:
            traces_of(0)
        if pair + 1 < ROWS_HERE // 2:
            traces_of(pair + 1)
        correlate(pair)

    rest = kept[pl.ds(16, WINDOWS, stride=KEPT), :]
    for block in range(1, 8):
        rest += kept[pl.ds(16 + block, WINDOWS, stride=KEPT), :]
    rest = rest.T
    own, cross = rest[:LMAX], rest[64 : 64 + LMAX]
    for lag in reversed(range(LMAX)):
        lines = kept[pl.ds(lag, WINDOWS, stride=KEPT), :].T
        own = own + lines[:LMAX]
        cross = cross + lines[64 : 64 + LMAX]
        place = LMAX - 1 - lag
        columns_at[pl.ds(place * 32, LMAX), :] = jnp.zeros((LMAX, WIN), jnp.float32)
        columns_at[pl.ds(place * 32 + place, LMAX), :] = own
        correl_at[pl.ds(place, 1), :] = cross[lag : lag + 1]
    energy = own[:1]
    step_size = 0.4 / (energy + 1e-06)
    places = lax.broadcasted_iota(jnp.int32, (LMAX, WIN), 0)
    tap_mask = (LMAX - 1 - places < length_ref[...]).astype(jnp.float32)
    correl = correl_at[...]
    matrix = []
    for lag in range(LMAX):
        place = LMAX - 1 - lag
        upper = columns_at[pl.ds(place * 32, LMAX), :]
        lower = columns_at[pl.ds(place, LMAX, stride=32), :]
        matrix.append(jnp.where(places < place, lower, upper))
    taps = (places == LMAX - 1).astype(jnp.float32)
    change = jnp.zeros((LMAX, WIN), jnp.float32)
    for sweep in range(FIT_STEPS):
        if sweep == 0:
            covered = matrix[0]
        else:
            covered = jnp.zeros((LMAX, WIN), jnp.float32)
            for lag in range(LMAX):
                place = LMAX - 1 - lag
                covered += matrix[lag] * jnp.broadcast_to(taps[place : place + 1], (LMAX, WIN))
        update = step_size * ((correl - covered) * tap_mask)
        taps = taps + update
        change = change + update
    high = change.astype(jnp.bfloat16).astype(jnp.float32)
    low = change - high
    gap = jnp.zeros((48, WIN), jnp.float32)
    filters[...] = jnp.concatenate([gap, low, gap, high], axis=0).T

    lanes = lax.broadcasted_iota(jnp.int32, (16, WIN), 1)
    samples = lax.broadcasted_iota(jnp.int32, (16, WIN), 0)
    inside = (lanes % WT) <= samples

    def subtract():
        for index in range(WINDOWS):
            row, start = window_at(index)
            ahead = field[row, pl.ds(start, WT), :]
            line = jnp.broadcast_to(filters[pl.ds(index, 1), :], (WT, WIN))
            turned = pltpu.roll(line, 1, 1, stride=1, stride_axis=0)
            turned = jnp.concatenate([jnp.where(inside, turned[:16], 0.0), turned[16:]], axis=0)
            shaped = jnp.dot(
                turned.astype(jnp.bfloat16),
                jnp.concatenate([ahead, ahead], axis=0),
                preferred_element_type=jnp.float32,
            )
            left = recorded_ref[index].astype(jnp.float32) - ahead.astype(jnp.float32)
            out_ref[target_ref[index]] = (left - shaped).astype(jnp.bfloat16)

    subtract()


def fit(target, parts, recorded, lengths, table, slots):
    whole = pl.BlockSpec(memory_space=pltpu.VMEM)
    return pl.pallas_call(
        fit_kernel,
        in_specs=[pl.BlockSpec(memory_space=pltpu.SMEM)] + [whole] * 4,
        out_specs=whole,
        out_shape=jax.ShapeDtypeStruct((slots, WT, WIN), jnp.bfloat16),
        scratch_shapes=[
            pltpu.VMEM((256, WIN), jnp.float32),
            pltpu.VMEM((ROWS_HERE // 2, 96, 2 * WIN), jnp.bfloat16),
            pltpu.VMEM((ROWS_HERE, 2 * NT, WIN), jnp.bfloat16),
            pltpu.VMEM((WINDOWS * KEPT, WIN), jnp.float32),
            pltpu.VMEM((LMAX * 32, WIN), jnp.float32),
            pltpu.VMEM((LMAX, WIN), jnp.float32),
            pltpu.VMEM((WINDOWS, WIN), jnp.float32),
        ],
        compiler_params=pltpu.CompilerParams(vmem_limit_bytes=40 * 1024 * 1024),
        name="fit",
    )(target, parts, recorded, lengths, table)


def drain_kernel(given_ref, out_ref, done):
    share = given_ref.shape[0] // DRAINS
    copies = [
        pltpu.make_async_copy(
            given_ref.at[pl.ds(part * share, share)],
            out_ref.at[pl.ds(part * share, share)],
            done.at[part],
        )
        for part in range(DRAINS)
    ]
    for copy in copies:
        copy.start()
    for copy in copies:
        copy.wait()


def drained(value):
    return pl.pallas_call(
        drain_kernel,
        in_specs=[pl.BlockSpec(memory_space=pltpu.VMEM)],
        out_specs=pl.BlockSpec(memory_space=pltpu.HBM),
        out_shape=jax.ShapeDtypeStruct(value.shape, value.dtype),
        scratch_shapes=[pltpu.SemaphoreType.DMA((DRAINS,))],
        compiler_params=pltpu.CompilerParams(vmem_limit_bytes=1024 * 1024),
        name="drain",
    )(value)


def moved(value, target_of):
    pairs = [(at, target_of(at)) for at in range(lax.axis_size("row"))]
    return lax.ppermute(value, "row", pairs)


def rows_of_panel(mine):
    peers = lax.axis_size("row")
    own = [mine] + [moved(mine, lambda at, by=by: (at + by) % peers) for by in (2, 4, 6)]
    other = [moved(piece, lambda at: at ^ 1) for piece in own]
    return [piece for pair in zip(own, other) for piece in pair]


def slot_of(owners, slots_each):
    count = owners.shape[0]
    same = owners[:, None] == owners[None, :]
    earlier = jnp.arange(count)[None, :] < jnp.arange(count)[:, None]
    return owners * slots_each + jnp.sum(jnp.logical_and(same, earlier), axis=1, dtype=jnp.int32)


def local(source_rows, data_matrix, observed, window_owner, filter_len):
    devices = lax.axis_size("freq") * lax.axis_size("row") * lax.axis_size("col")
    mark = marker()
    partial = predict(rows_of_panel(source_rows), data_matrix, mark)
    parts = lax.all_to_all(partial, ("freq", "col"), 0, 0, tiled=True)
    recorded = (
        observed.reshape(NT // WT, WT, ROWS_HERE, WIN).transpose(2, 0, 1, 3).reshape(-1, WT, WIN)
    )
    target = slot_of(window_owner.reshape(-1), 2)
    buffer = fit(
        target,
        parts,
        recorded,
        filter_len.reshape(1, -1),
        jnp.asarray(table_parts(BANDS, NT)),
        devices * 2,
    )
    result = lax.all_to_all(
        buffer.reshape(devices, 2, WT, WIN), ("freq", "row", "col"), 0, 0, tiled=True
    )
    return drained(result)[None]


def solution(mesh):
    return jax.shard_map(
        local,
        mesh=mesh,
        in_specs=(
            P(None, "freq", "row", "col"),
            P(None, "freq", "col", "row"),
            P(None, "freq", ("row", "col")),
            P("freq", ("row", "col"), None, None),
            P("freq", ("row", "col"), None),
        ),
        out_specs=P(("freq", "row", "col"), None, None, None, None),
        check_vma=False,
    )
```
